1024 devices in a mesh: row: 64 (over y, x), col: 16 (over z, core).
Axes of the slice: x: 8, y: 8, z: 8, core: 2. Of those that a mesh axis runs over, the one named last changes fastest.
Arguments:
- tokens: bfloat16 [64, 32, 32, 2048], P('row', None, None, 'col'), may hold values from -120 to 120
- turns: int32 [64, 4], replicated, may hold values from 0 to 7
- dw_weight: float32 [49, 2048], P(None, 'col'), may hold values from -0.875 to 0.875
- dw_bias: float32 [2048], P('col'), may hold values from -3 to 3
- ln_gain: float32 [2048], P('col'), may hold values from 0.1 to 1.9
- ln_bias: float32 [2048], P('col'), may hold values from -2 to 2
- w_in: bfloat16 [2048, 8192], P('row', 'col'), may hold values from -0.125 to 0.125
- b_in: float32 [8192], P('col'), may hold values from -3 to 3
Outputs:
- activations: bfloat16 [64, 32, 32, 8192], P('row', None, None, 'col')
The draws below stay inside these ranges and needn't reach their ends.
All inputs are finite; a program needn't handle non-finite values.
Results may differ from the reference program's by a relative error of at most 0.0047.
Values may be sent and summed in bfloat16 or wider, within the bound.
A program may use at most 32 MiB of HBM per device.

```python
import jax
import jax.numpy as jnp
from jax import lax

D = 2048
FF = 8192
KERNEL = 7
P_SIZE = 32
PATCHES = 64
CYCLE = 8


def draw_tokens(key, part):
    keys = jax.random.split(jax.random.fold_in(key, 11), 2)
    shape = (PATCHES, P_SIZE, P_SIZE, D)
    ramp = jnp.exp(jnp.log(3.0) * jnp.arange(D, dtype=jnp.float32) / (D - 1))
    spread = jnp.exp(jax.random.uniform(keys[1], (D,), jnp.float32, 0.0, jnp.log(10.0)))
    base = jnp.clip(jax.random.normal(keys[0], shape, jnp.float32), -4.0, 4.0)
    return (base * ramp * spread / 5.0).astype(jnp.bfloat16)


def with_ends(array, key, least, top_value):
    longest = array.shape.index(max(array.shape))
    spots = []
    for shift in (0, 1):
        where = [jax.random.randint(jax.random.fold_in(key, axis), (), 0, length) for axis, length in enumerate(array.shape)]
        where[longest] = (where[longest] + shift) % array.shape[longest]
        spots.append(tuple(where))
    return array.at[spots[0]].set(least).at[spots[1]].set(top_value)


def level_of(stream_key, dims, shards, least, high):
    factor_of = 1.0
    for axis_at, blocks in shards:
        draws = jax.random.uniform(jax.random.fold_in(jax.random.fold_in(stream_key, 6), axis_at), (blocks,), jnp.float32, least / len(shards), high / len(shards))
        factor_of = factor_of * jnp.repeat(jnp.exp(draws), dims[axis_at] // blocks).reshape((-1,) + (1,) * (len(dims) - 1 - axis_at))
    return factor_of


def bell_draw(stream_key, dims, scale, limit, cuts=(), held_as=jnp.bfloat16):
    factor_of = level_of(stream_key, dims, cuts, -0.22, 0.18) if cuts else 1.0
    values = jax.random.normal(stream_key, dims, jnp.float32) * scale * factor_of
    return jnp.minimum(jnp.maximum(values, -limit), limit).astype(held_as)


def setup_inputs(seed: int = 0) -> dict:
    streams_of = jax.random.split(jax.random.key(seed), 9)
    return {
        "tokens": draw_tokens(jax.random.fold_in(streams_of[8], 71), 0),
        "turns": with_ends(jax.random.randint(streams_of[1], (PATCHES, 4), 0, 8), jax.random.fold_in(streams_of[1], 1), 0, 7).astype(jnp.int32),
        "dw_weight": bell_draw(streams_of[2], (KERNEL * KERNEL, D), (KERNEL * KERNEL) ** -0.5, 0.875, ((1, 16),), jnp.float32),
        "dw_bias": bell_draw(streams_of[3], (D,), 0.5, 3.0, ((0, 16),), jnp.float32),
        "ln_gain": jnp.clip(1.0 + 0.18 * jax.random.normal(streams_of[4], (D,), jnp.float32), 0.1, 1.9),
        "ln_bias": bell_draw(streams_of[5], (D,), 0.3, 2.0, ((0, 16),), jnp.float32),
        "w_in": bell_draw(streams_of[6], (D, FF), D ** -0.5, 0.125, ((0, 64), (1, 16))),
        "b_in": bell_draw(streams_of[7], (FF,), 0.5, 3.0, ((0, 16),), jnp.float32),
    }


def side_strips(pixels):
    first = pixels[:, 0:3]
    second = jnp.swapaxes(pixels[:, :, ::-1][:, :, 0:3], 1, 2)
    third = pixels[:, ::-1][:, 0:3]
    fourth = jnp.swapaxes(pixels[:, :, 0:3], 1, 2)
    return jnp.stack([first, second, third, fourth], axis=1)

def assemble(pixels, ghosts):
    upper = ghosts[0][:, ::-1]
    lower = ghosts[2]
    right_side = jnp.swapaxes(ghosts[1], 1, 2)
    left_side = jnp.swapaxes(ghosts[3][:, ::-1], 1, 2)
    corner = jnp.zeros((pixels.shape[0], 3, 3, pixels.shape[3]), pixels.dtype)
    upper_band = jnp.concatenate([corner, upper, corner], axis=2)
    middle_band = jnp.concatenate([left_side, pixels, right_side], axis=2)
    lower_band = jnp.concatenate([corner, lower, corner], axis=2)
    return jnp.concatenate([upper_band, middle_band, lower_band], axis=1)

def reference(tokens, turns, dw_weight, dw_bias, ln_gain, ln_bias, w_in, b_in):
    patches = tokens.shape[0]
    strips = side_strips(tokens)
    offsets = [-CYCLE, 1, CYCLE, -1]
    ghosts = []
    for side in range(4):
        source = (jnp.arange(patches, dtype=jnp.int32) + offsets[side]) % patches
        turn_code = turns[:, side]
        chosen_side = (side + 2 + turn_code) % 4
        taken = strips[source, chosen_side]
        flipped = (turn_code // 4 == 1)[:, None, None, None]
        ghosts.append(jnp.where(flipped, taken[:, :, ::-1], taken))

    def one_patch(patch_items):
        pixels, ghost_top, ghost_right, ghost_bottom, ghost_left = patch_items
        padded = assemble(pixels[None], [ghost_top[None], ghost_right[None], ghost_bottom[None], ghost_left[None]])[0]
        padded = padded.astype(jnp.float32)
        summed = jnp.zeros((P_SIZE, P_SIZE, D), jnp.float32)
        for row_off in range(KERNEL):
            for col_off in range(KERNEL):
                summed = summed + padded[row_off:row_off + P_SIZE, col_off:col_off + P_SIZE] * dw_weight[row_off * KERNEL + col_off]
        conv = summed + dw_bias
        centre_mean = lax.optimization_barrier(jnp.sum(conv, axis=-1, keepdims=True)) / D
        variance = lax.optimization_barrier(jnp.sum(conv * conv, axis=-1, keepdims=True)) / D - centre_mean * centre_mean
        normed = ((conv - centre_mean) * lax.rsqrt(variance + 1e-06) * ln_gain + ln_bias).astype(jnp.bfloat16)
        preact = jnp.dot(normed.reshape(P_SIZE * P_SIZE, D), w_in, preferred_element_type=jnp.float32) + b_in
        return jax.nn.gelu(preact, approximate=False).astype(jnp.bfloat16).reshape(P_SIZE, P_SIZE, FF)
    return lax.map(one_patch, (tokens, ghosts[0], ghosts[1], ghosts[2], ghosts[3]))
```

```python
import functools

import jax
import jax.numpy as jnp
from jax import lax
from jax.experimental import pallas as pl
from jax.experimental.pallas import tpu as pltpu
from jax.sharding import PartitionSpec as P

D = 2048
KERNEL = 7
SIDE = 32
CH = 128
HID = 512
HALF = HID // 2
PITCH = 48
LEFT = 8
RING = 8
NC = 4
CROWS = SIDE // NC
PX = SIDE * SIDE // NC
MESH = pl.DeviceIdType.MESH


def body(
    turns_ref, tok_hbm, dww_hbm, vec_hbm, bin_hbm, w_hbm, out_hbm,
    tok_v, dww_v, vec_v, bin_v, wexp, pad, sbuf, rbuf, conv_v,
    st_send, st_recv, act, acc, wa, wb, obuf,
    loc_sem, halo_s, halo_r, st_s, st_r, w1_s, w1_r, w2_s, w2_r,
    zp_s, zm_s, z_r, zr4, sib_s, sib_r, out_s,
):
    row = lax.axis_index("row")
    col = lax.axis_index("col")
    y, x = lax.div(row, RING), lax.rem(row, RING)
    z, core = lax.div(col, 2), lax.rem(col, 2)

    def wrap(v, n):
        return lax.rem(v, n)

    def remote(src, dst, ssem, rsem, dev):
        return pltpu.make_async_remote_copy(
            src_ref=src, dst_ref=dst, send_sem=ssem, recv_sem=rsem,
            device_id=dev, device_id_type=MESH,
        )

    x_peer = [(y * RING + wrap(x + k, RING), col) for k in range(RING)]
    y_peer = [(wrap(row + RING * k, 64), col) for k in range(RING)]
    z_line = [(row, wrap(col + k, 16)) for k in range(16)]
    up_z = (row, wrap(col + 2, 16))
    down_z = (row, wrap(col + 14, 16))
    sibling = (row, z * 2 + (1 - core))
    halo_dev = [
        (wrap(row + 8, 64), col),
        (wrap(row + 63, 64), col),
        (wrap(row + 56, 64), col),
        (wrap(row + 1, 64), col),
    ]
    peers = x_peer[1:] + y_peer[1:] + z_line[1:] + [halo_dev[1], halo_dev[3]]

    barrier = pltpu.get_barrier_semaphore()
    for dev in peers:
        pl.semaphore_signal(barrier, inc=1, device_id=dev, device_id_type=MESH)

    loads = [
        pltpu.make_async_copy(tok_hbm, tok_v, loc_sem.at[0]),
        pltpu.make_async_copy(dww_hbm, dww_v, loc_sem.at[1]),
        pltpu.make_async_copy(vec_hbm, vec_v, loc_sem.at[2]),
        pltpu.make_async_copy(bin_hbm, bin_v, loc_sem.at[3]),
        pltpu.make_async_copy(w_hbm.at[:, 0:HALF], wa.at[y, x], loc_sem.at[4]),
        pltpu.make_async_copy(w_hbm.at[:, HALF:HID], wb.at[y, x], loc_sem.at[5]),
    ]
    for c in loads:
        c.start()

    zero_rows = jnp.zeros((3 * PITCH, CH), jnp.float32)
    pad[0 : 3 * PITCH, :] = zero_rows
    pad[35 * PITCH : 38 * PITCH, :] = zero_rows

    loads[0].wait()
    for i in range(SIDE):
        pad[(3 + i) * PITCH + LEFT : (3 + i) * PITCH + LEFT + SIDE, :] = tok_v[
            i * SIDE : (i + 1) * SIDE, :
        ].astype(jnp.float32)

    strips = [[], [], [], []]
    for d in range(3):
        strips[0].append(pad[pl.ds((3 + d) * PITCH + LEFT, SIDE), :])
        strips[1].append(pad[pl.ds(3 * PITCH + LEFT + 31 - d, SIDE, stride=PITCH), :])
        strips[2].append(pad[pl.ds((34 - d) * PITCH + LEFT, SIDE), :])
        strips[3].append(pad[pl.ds(3 * PITCH + LEFT + d, SIDE, stride=PITCH), :])
    chosen = []
    codes = []
    for s in range(4):
        code = turns_ref[s, halo_dev[s][0]]
        codes.append(code)
        k = lax.rem(s + 2 + code, 4)
        for d in range(3):
            chosen.append(
                jnp.where(
                    k == 0,
                    strips[0][d],
                    jnp.where(k == 1, strips[1][d], jnp.where(k == 2, strips[2][d], strips[3][d])),
                )
            )
    flip = (
        lax.broadcasted_iota(jnp.int32, (SIDE, SIDE), 0)
        + lax.broadcasted_iota(jnp.int32, (SIDE, SIDE), 1)
        == SIDE - 1
    )
    flip = jnp.where(flip, 1.0, 0.0).astype(jnp.bfloat16)
    side_by_side = jnp.concatenate(chosen, axis=1)
    flipped = jnp.dot(
        flip, side_by_side.astype(jnp.bfloat16), preferred_element_type=jnp.float32
    )
    for s in range(4):
        for d in range(3):
            q = 3 * s + d
            sbuf[s, d * SIDE : (d + 1) * SIDE, :] = jnp.where(
                codes[s] >= 4, flipped[:, q * CH : (q + 1) * CH], chosen[q]
            ).astype(jnp.bfloat16)

    pl.semaphore_wait(barrier, len(peers))

    halo = [
        remote(sbuf.at[s], rbuf.at[s], halo_s.at[s], halo_r.at[s], halo_dev[s])
        for s in range(4)
    ]
    for c in halo:
        c.start()
    loads[4].wait()
    loads[5].wait()
    w_first = []
    for k in range(1, RING):
        w_first.append(
            remote(wa.at[y, x], wa.at[y, x], w1_s.at[0, k - 1], w1_r.at[0, k - 1], x_peer[k])
        )
        w_first.append(
            remote(wb.at[y, x], wb.at[y, x], w1_s.at[1, k - 1], w1_r.at[1, k - 1], y_peer[k])
        )
    for c in w_first:
        c.start()

    loads[1].wait()
    loads[2].wait()
    loads[3].wait()
    for k in range(KERNEL * KERNEL):
        wexp[k] = jnp.broadcast_to(dww_v[k : k + 1, :], (8, CH))

    def w_group(which, g):
        return wa.at[g] if which == 0 else wb.at[:, g]

    def w_part(which, g, part):
        if which == 0:
            return wa.at[g, 4 * part : 4 * part + 4]
        return wb.at[4 * part : 4 * part + 4, g]

    here = (y, x)
    ahead = (y_peer[1], x_peer[1])
    behind = (y_peer[7], x_peer[7])

    def w_send(which, forward, hop):
        off = hop - 1
        if forward:
            g = wrap(here[which] + RING - off, RING)
            dev, lane = ahead[which], 0
        else:
            g = wrap(here[which] + off, RING)
            dev, lane = behind[which], 1
        ref = w_group(which, g) if hop < 4 else w_part(which, g, lane)
        return remote(
            ref, ref, w2_s.at[which, lane, hop - 1], w2_r.at[which, lane, hop - 1], dev
        )

    def w_step(hop):
        for which in range(2):
            for forward in (True, False):
                if hop > 1:
                    w_send(which, forward, hop - 1).wait_recv()
                if hop <= 4:
                    w_send(which, forward, hop).start()

    for s in range(4):
        halo[s].wait_recv()
    for d in range(3):
        pad[pl.ds((2 - d) * PITCH + LEFT, SIDE), :] = rbuf[
            0, d * SIDE : (d + 1) * SIDE, :
        ].astype(jnp.float32)
        pad[pl.ds((35 + d) * PITCH + LEFT, SIDE), :] = rbuf[
            2, d * SIDE : (d + 1) * SIDE, :
        ].astype(jnp.float32)
        pad[pl.ds(3 * PITCH + LEFT + SIDE + d, SIDE, stride=PITCH), :] = rbuf[
            1, d * SIDE : (d + 1) * SIDE, :
        ].astype(jnp.float32)
        pad[pl.ds(3 * PITCH + LEFT - 1 - d, SIDE, stride=PITCH), :] = rbuf[
            3, d * SIDE : (d + 1) * SIDE, :
        ].astype(jnp.float32)

    bias = jnp.broadcast_to(vec_v[0:1, :], (8, CH))
    lane_id = lax.broadcasted_iota(jnp.int32, (8, CH), 1)

    def conv_chunk(c, sums):
        def block(jb, carry):
            s1, s2 = carry
            total = [bias] * CROWS
            for b in range(KERNEL):
                taps = [wexp[a * KERNEL + b] for a in range(KERNEL)]
                for r in range(CROWS + KERNEL - 1):
                    start = (c * CROWS + r) * PITCH + LEFT - 3 + b + jb * 8
                    line = pad[pl.ds(start, 8), :]
                    for a in range(max(0, r - CROWS + 1), min(KERNEL - 1, r) + 1):
                        total[r - a] = total[r - a] + line * taps[a]
            for r in range(CROWS):
                i = c * CROWS + r
                at = pl.multiple_of(i * SIDE + jb * 8, 8)
                conv_v[pl.ds(at, 8), :] = total[r]
                here_lane = lane_id == 4 * i + jb
                s1 = jnp.where(here_lane, jnp.sum(total[r], axis=1, keepdims=True), s1)
                s2 = jnp.where(here_lane, jnp.sum(total[r] * total[r], axis=1, keepdims=True), s2)
            return s1, s2

        return lax.fori_loop(0, SIDE // 8, block, sums)

    def stats_copy(half, k):
        return remote(
            st_send.at[half], st_recv.at[half, k - 1], st_s.at[half, k - 1],
            st_r.at[half, k - 1], z_line[k],
        )

    zero = jnp.zeros((8, CH), jnp.float32)
    for half in range(2):
        sums = (zero, zero)
        for c in (2 * half, 2 * half + 1):
            sums = conv_chunk(c, sums)
        st_send[half, 0] = sums[0]
        st_send[half, 1] = sums[1]
        for k in range(1, 16):
            stats_copy(half, k).start()

    for c in w_first:
        c.wait_recv()
    w_step(1)

    def block_of(c, off):
        return act.at[c, 2 * wrap(z + RING - off, RING) + core]

    def sib_block(c, off):
        return act.at[c, 2 * wrap(z + RING - off, RING) + 1 - core]

    HP = PX // 2

    def z_forward(c, off):
        ref = block_of(c, off)
        if off == 3:
            ref = ref.at[0:HP]
            return remote(ref, ref, zp_s.at[c, off], zr4.at[c, 0], up_z)
        return remote(ref, ref, zp_s.at[c, off], z_r.at[c, off], up_z)

    def z_backward(c, off):
        ref = block_of(c, RING - off if off else 0)
        if off == 3:
            ref = ref.at[HP:PX]
            return remote(ref, ref, zm_s.at[c, off], zr4.at[c, 1], down_z)
        return remote(ref, ref, zm_s.at[c, off], z_r.at[c, 3 + off], down_z)

    def sib_send(c, off):
        ref = block_of(c, off)
        return remote(ref, ref, sib_s.at[c, off], sib_r.at[c, off], sibling)

    gain = jnp.broadcast_to(vec_v[1:2, :], (8, CH))
    shift = jnp.broadcast_to(vec_v[2:3, :], (8, CH))

    for half in range(2):
        s1 = st_send[half, 0]
        s2 = st_send[half, 1]
        for k in range(1, 16):
            stats_copy(half, k).wait_recv()
            s1 = s1 + st_recv[half, k - 1, 0]
            s2 = s2 + st_recv[half, k - 1, 1]
        mean = s1 / D
        rstd = lax.rsqrt(s2 / D - mean * mean + 1e-06)
        for c in (2 * half, 2 * half + 1):
            for q in range(PX // 16):
                parts = []
                for h in range(2):
                    lane = c * (PX // 8) + 2 * q + h
                    m = jnp.broadcast_to(mean[:, lane : lane + 1], (8, CH))
                    r = jnp.broadcast_to(rstd[:, lane : lane + 1], (8, CH))
                    v = conv_v[lane * 8 : lane * 8 + 8, :]
                    parts.append((v - m) * r * gain + shift)
                act[c, col, 16 * q : 16 * q + 16, :] = jnp.concatenate(parts, axis=0).astype(
                    jnp.bfloat16
                )
            z_forward(c, 0).start()
            z_backward(c, 0).start()
            sib_send(c, 0).start()

    w_step(2)

    def relay(hop):
        def one(c, _):
            if hop < 4:
                z_forward(c, hop - 1).wait_recv()
                z_forward(c, hop).start()
                sib_send(c, hop).start()
                z_backward(c, hop - 1).wait_recv()
                z_backward(c, hop).start()
                sib_send(c, RING - hop).start()
            else:
                z_forward(c, 3).wait_recv()
                z_backward(c, 3).wait_recv()
                sib_send(c, 4).start()
            return 0

        lax.fori_loop(0, NC, one, 0)

    def lhs(c, off):
        src = wrap(z + RING - off, RING)
        return [act[c, 2 * src], act[c, 2 * src + 1]]

    def rhs(ref, off):
        src = wrap(z + RING - off, RING)
        return ref[src].reshape(RING * SIDE, HALF)

    def multiply(offs, first):
        def one(c, _):
            for off in offs:
                sib_send(c, off).wait_recv()
            left = []
            for off in offs:
                left += lhs(c, off)
            left = jnp.concatenate(left, axis=1)
            for which, ref in ((0, wa), (1, wb)):
                right = jnp.concatenate([rhs(ref, off) for off in offs], axis=0)
                prod = jnp.dot(left, right, preferred_element_type=jnp.float32)
                lanes = slice(which * HALF, (which + 1) * HALF)
                if first:
                    acc[c, :, lanes] = prod
                else:
                    acc[c, :, lanes] += prod
            return 0

        lax.fori_loop(0, NC, one, 0)

    relay(1)
    w_step(3)
    relay(2)
    w_step(4)
    relay(3)
    w_step(5)
    multiply([0, 1, 7], True)
    multiply([2, 6], False)
    relay(4)
    multiply([3, 5], False)

    hidden_bias = bin_v[0:1, :]

    def finish(c, _):
        sib_send(c, 4).wait_recv()
        left = jnp.concatenate(lhs(c, 4), axis=1)
        for which, ref in ((0, wa), (1, wb)):
            lanes = slice(which * HALF, (which + 1) * HALF)
            acc[c, :, lanes] += jnp.dot(left, rhs(ref, 4), preferred_element_type=jnp.float32)

        def rows(i, _):
            at = pl.ds(pl.multiple_of(i * 16, 16), 16)
            v = acc[c, at, :] + hidden_bias
            obuf[c, at, :] = (0.5 * v * (1.0 + lax.erf(v * 0.7071067811865476))).astype(
                jnp.bfloat16
            )
            return 0

        lax.fori_loop(0, PX // 16, rows, 0)
        pltpu.make_async_copy(
            obuf.at[c], out_hbm.at[pl.ds(pl.multiple_of(c * PX, PX), PX)], out_s.at[c]
        ).start()
        return 0

    lax.fori_loop(0, NC, finish, 0)

    for c in halo:
        c.wait_send()
    for c in w_first:
        c.wait_send()
    for hop in range(1, 5):
        for which in range(2):
            w_send(which, True, hop).wait_send()
            w_send(which, False, hop).wait_send()
    for half in range(2):
        for k in range(1, 16):
            stats_copy(half, k).wait_send()

    def drain(c, _):
        for off in range(4):
            z_forward(c, off).wait_send()
            z_backward(c, off).wait_send()
        for off in range(RING):
            sib_send(c, off).wait_send()
        pltpu.make_async_copy(
            obuf.at[c], out_hbm.at[pl.ds(pl.multiple_of(c * PX, PX), PX)], out_s.at[c]
        ).wait()
        return 0

    lax.fori_loop(0, NC, drain, 0)


def per_device(tokens, turns, dw_weight, dw_bias, ln_gain, ln_bias, w_in, b_in):
    pixels = SIDE * SIDE
    vectors = jnp.stack([dw_bias, ln_gain, ln_bias])
    anywhere = pl.BlockSpec(memory_space=pl.ANY)
    dma = pltpu.SemaphoreType.DMA
    out = pl.pallas_call(
        body,
        name="block",
        out_shape=jax.ShapeDtypeStruct((pixels, HID), jnp.bfloat16),
        in_specs=[pl.BlockSpec(memory_space=pltpu.SMEM)] + [anywhere] * 5,
        out_specs=anywhere,
        scratch_shapes=[
            pltpu.VMEM((pixels, CH), jnp.bfloat16),
            pltpu.VMEM((KERNEL * KERNEL, CH), jnp.float32),
            pltpu.VMEM((3, CH), jnp.float32),
            pltpu.VMEM((1, HID), jnp.float32),
            pltpu.VMEM((KERNEL * KERNEL, 8, CH), jnp.float32),
            pltpu.VMEM((38 * PITCH, CH), jnp.float32),
            pltpu.VMEM((4, 3 * SIDE, CH), jnp.bfloat16),
            pltpu.VMEM((4, 3 * SIDE, CH), jnp.bfloat16),
            pltpu.VMEM((pixels, CH), jnp.float32),
            pltpu.VMEM((2, 2, 8, CH), jnp.float32),
            pltpu.VMEM((2, 15, 2, 8, CH), jnp.float32),
            pltpu.VMEM((NC, 16, PX, CH), jnp.bfloat16),
            pltpu.VMEM((NC, PX, HID), jnp.float32),
            pltpu.VMEM((RING, RING, 32, HALF), jnp.bfloat16),
            pltpu.VMEM((RING, RING, 32, HALF), jnp.bfloat16),
            pltpu.VMEM((NC, PX, HID), jnp.bfloat16),
            dma((6,)),
            dma((4,)), dma((4,)),
            dma((2, 15)), dma((2, 15)),
            dma((2, 7)), dma((2, 7)),
            dma((2, 2, 4)), dma((2, 2, 4)),
            dma((NC, 4)), dma((NC, 4)), dma((NC, 6)), dma((NC, 2)),
            dma((NC, RING)), dma((NC, RING)),
            dma((NC,)),
        ],
        compiler_params=pltpu.CompilerParams(
            collective_id=0, has_side_effects=True, vmem_limit_bytes=40 * 1024 * 1024
        ),
    )(
        turns.T,
        tokens.reshape(pixels, CH),
        dw_weight,
        vectors,
        b_in.reshape(1, HID),
        w_in,
    )
    return out.reshape(1, SIDE, SIDE, HID)


def solution(mesh):
    in_specs = (
        P("row", None, None, "col"),
        P(),
        P(None, "col"),
        P("col"),
        P("col"),
        P("col"),
        P("row", "col"),
        P("col"),
    )
    out_specs = P("row", None, None, "col")
    return jax.shard_map(
        per_device, mesh=mesh, in_specs=in_specs, out_specs=out_specs, check_vma=False
    )
```

```python
import functools

import jax
import jax.numpy as jnp
from jax import lax
from jax.experimental import pallas as pl
from jax.experimental.pallas import tpu as pltpu
from jax.sharding import PartitionSpec as P

D = 2048
KERNEL = 7
SIDE = 32
CH = 128
HID = 512
HALF = HID // 2
PITCH = 48
LEFT = 8
RING = 8
NC = 4
CROWS = SIDE // NC
PX = SIDE * SIDE // NC
MESH = pl.DeviceIdType.MESH


def body(
    turns_hbm, tok_hbm, dww_hbm, bias_hbm, gain_hbm, shift_hbm, bin_hbm, w_hbm, out_hbm,
    turns_ref, tok_v, dww_v, vec_v, bin_v, wexp, pad, sbuf, rbuf, conv_v,
    st_send, st_pair, st_chip, st_recv, act, acc, wa, wb, obuf,
    loc_sem, halo_s, halo_r, pair_s, pair_r, st_s, st_r, w1_s, w1_r, w2_s, w2_r,
    zp_s, zm_s, z_r, zr4, sib_s, sib_r, out_s,
):
    row = lax.axis_index("row")
    col = lax.axis_index("col")
    y, x = lax.div(row, RING), lax.rem(row, RING)
    z, core = lax.div(col, 2), lax.rem(col, 2)

    def wrap(v, n):
        return lax.rem(v, n)

    def remote(src, dst, ssem, rsem, dev):
        return pltpu.make_async_remote_copy(
            src_ref=src, dst_ref=dst, send_sem=ssem, recv_sem=rsem,
            device_id=dev, device_id_type=MESH,
        )

    x_peer = [(y * RING + wrap(x + k, RING), col) for k in range(RING)]
    y_peer = [(wrap(row + RING * k, 64), col) for k in range(RING)]
    z_line = [(row, wrap(col + k, 16)) for k in range(16)]
    up_z = (row, wrap(col + 2, 16))
    down_z = (row, wrap(col + 14, 16))
    sibling = (row, z * 2 + (1 - core))
    halo_dev = [
        (wrap(row + 8, 64), col),
        (wrap(row + 63, 64), col),
        (wrap(row + 56, 64), col),
        (wrap(row + 1, 64), col),
    ]
    peers = x_peer[1:] + y_peer[1:] + z_line[2::2] + [sibling, halo_dev[1], halo_dev[3]]

    barrier = pltpu.get_barrier_semaphore()
    for dev in peers:
        pl.semaphore_signal(barrier, inc=1, device_id=dev, device_id_type=MESH)

    loads = [
        pltpu.make_async_copy(tok_hbm, tok_v, loc_sem.at[0]),
        pltpu.make_async_copy(dww_hbm, dww_v, loc_sem.at[1]),
        pltpu.make_async_copy(bias_hbm, vec_v.at[0:1], loc_sem.at[2]),
        pltpu.make_async_copy(bin_hbm, bin_v, loc_sem.at[3]),
        pltpu.make_async_copy(w_hbm.at[:, 0:HALF], wa.at[y, x], loc_sem.at[4]),
        pltpu.make_async_copy(w_hbm.at[:, HALF:HID], wb.at[y, x], loc_sem.at[5]),
        pltpu.make_async_copy(gain_hbm, vec_v.at[1:2], loc_sem.at[6]),
        pltpu.make_async_copy(shift_hbm, vec_v.at[2:3], loc_sem.at[7]),
        pltpu.make_async_copy(turns_hbm, turns_ref, loc_sem.at[8]),
    ]
    for c in loads:
        c.start()

    zero_rows = jnp.zeros((3 * PITCH, CH), jnp.float32)
    pad[0 : 3 * PITCH, :] = zero_rows
    pad[35 * PITCH : 38 * PITCH, :] = zero_rows

    loads[0].wait()
    loads[8].wait()
    for i in range(SIDE):
        pad[(3 + i) * PITCH + LEFT : (3 + i) * PITCH + LEFT + SIDE, :] = tok_v[
            i * SIDE : (i + 1) * SIDE, :
        ].astype(jnp.float32)

    strips = [[], [], [], []]
    for d in range(3):
        strips[0].append(pad[pl.ds((3 + d) * PITCH + LEFT, SIDE), :])
        strips[1].append(pad[pl.ds(3 * PITCH + LEFT + 31 - d, SIDE, stride=PITCH), :])
        strips[2].append(pad[pl.ds((34 - d) * PITCH + LEFT, SIDE), :])
        strips[3].append(pad[pl.ds(3 * PITCH + LEFT + d, SIDE, stride=PITCH), :])
    chosen = []
    codes = []
    for s in range(4):
        code = turns_ref[s, halo_dev[s][0]]
        codes.append(code)
        k = lax.rem(s + 2 + code, 4)
        for d in range(3):
            chosen.append(
                jnp.where(
                    k == 0,
                    strips[0][d],
                    jnp.where(k == 1, strips[1][d], jnp.where(k == 2, strips[2][d], strips[3][d])),
                )
            )
    flip = (
        lax.broadcasted_iota(jnp.int32, (SIDE, SIDE), 0)
        + lax.broadcasted_iota(jnp.int32, (SIDE, SIDE), 1)
        == SIDE - 1
    )
    flip = jnp.where(flip, 1.0, 0.0).astype(jnp.bfloat16)
    side_by_side = jnp.concatenate(chosen, axis=1)
    flipped = jnp.dot(
        flip, side_by_side.astype(jnp.bfloat16), preferred_element_type=jnp.float32
    )
    for s in range(4):
        for d in range(3):
            q = 3 * s + d
            sbuf[s, d * SIDE : (d + 1) * SIDE, :] = jnp.where(
                codes[s] >= 4, flipped[:, q * CH : (q + 1) * CH], chosen[q]
            ).astype(jnp.bfloat16)

    pl.semaphore_wait(barrier, len(peers))

    halo = [
        remote(sbuf.at[s], rbuf.at[s], halo_s.at[s], halo_r.at[s], halo_dev[s])
        for s in range(4)
    ]
    for c in halo:
        c.start()
    here = (y, x)
    ahead = (y_peer[1], x_peer[1])
    behind = (y_peer[7], x_peer[7])

    def w1_send(which, k):
        ref = wa.at[y, x] if which == 0 else wb.at[y, x]
        dev = x_peer[k] if which == 0 else y_peer[k]
        return remote(ref, ref, w1_s.at[which, k - 1], w1_r.at[which, k - 1], dev)

    def w_group(which, g):
        return wa.at[g] if which == 0 else wb.at[:, g]

    def w_part(which, g, part):
        if which == 0:
            return wa.at[g, 4 * part : 4 * part + 4]
        return wb.at[4 * part : 4 * part + 4, g]

    def w_send(which, forward, hop):
        off = hop - 1
        if forward:
            g = wrap(here[which] + RING - off, RING)
            dev, lane = ahead[which], 0
        else:
            g = wrap(here[which] + off, RING)
            dev, lane = behind[which], 1
        ref = w_group(which, g) if hop < 4 else w_part(which, g, lane)
        return remote(
            ref, ref, w2_s.at[which, lane, hop - 1], w2_r.at[which, lane, hop - 1], dev
        )

    def w_step(hop):
        for which in range(2):
            for forward in (True, False):
                if hop > 1:
                    w_send(which, forward, hop - 1).wait_recv()
                if hop <= 4:
                    w_send(which, forward, hop).start()

    loads[4].wait()
    loads[5].wait()
    for k in range(1, RING):
        w1_send(0, k).start()
        w1_send(1, k).start()

    loads[1].wait()
    loads[2].wait()
    loads[3].wait()
    loads[6].wait()
    loads[7].wait()
    for k in range(KERNEL * KERNEL):
        wexp[k] = jnp.broadcast_to(dww_v[k : k + 1, :], (8, CH))

    for s in range(4):
        halo[s].wait_recv()
    for d in range(3):
        pad[pl.ds((2 - d) * PITCH + LEFT, SIDE), :] = rbuf[
            0, d * SIDE : (d + 1) * SIDE, :
        ].astype(jnp.float32)
        pad[pl.ds((35 + d) * PITCH + LEFT, SIDE), :] = rbuf[
            2, d * SIDE : (d + 1) * SIDE, :
        ].astype(jnp.float32)
        pad[pl.ds(3 * PITCH + LEFT + SIDE + d, SIDE, stride=PITCH), :] = rbuf[
            1, d * SIDE : (d + 1) * SIDE, :
        ].astype(jnp.float32)
        pad[pl.ds(3 * PITCH + LEFT - 1 - d, SIDE, stride=PITCH), :] = rbuf[
            3, d * SIDE : (d + 1) * SIDE, :
        ].astype(jnp.float32)

    bias = jnp.broadcast_to(vec_v[0:1, :], (8, CH))
    lane_id = lax.broadcasted_iota(jnp.int32, (8, CH), 1)

    def conv_chunk(c, packed):
        def block(jb, packed):
            total = [bias] * CROWS
            for b in range(KERNEL):
                taps = [wexp[a * KERNEL + b] for a in range(KERNEL)]
                for r in range(CROWS + KERNEL - 1):
                    start = (c * CROWS + r) * PITCH + LEFT - 3 + b + jb * 8
                    line = pad[pl.ds(start, 8), :]
                    for a in range(max(0, r - CROWS + 1), min(KERNEL - 1, r) + 1):
                        total[r - a] = total[r - a] + line * taps[a]
            for r in range(CROWS):
                i = c * CROWS + r
                at = pl.multiple_of(i * SIDE + jb * 8, 8)
                conv_v[pl.ds(at, 8), :] = total[r]
                lane = (4 * i) % 64 + jb
                s1 = jnp.sum(total[r], axis=1, keepdims=True)
                s2 = jnp.sum(total[r] * total[r], axis=1, keepdims=True)
                packed = jnp.where(lane_id == lane, s1, packed)
                packed = jnp.where(lane_id == lane + 64, s2, packed)
            return packed

        return lax.fori_loop(0, SIDE // 8, block, packed)

    def pair_copy(half):
        return remote(
            st_send.at[half], st_pair.at[half], pair_s.at[half], pair_r.at[half], sibling
        )

    def stats_copy(half, k):
        return remote(
            st_chip.at[half], st_recv.at[half, k - 1], st_s.at[half, k - 1],
            st_r.at[half, k - 1], z_line[2 * k],
        )

    def send_chip_sums(half):
        pair_copy(half).wait_recv()
        st_chip[half] = st_send[half] + st_pair[half]
        for k in range(1, RING):
            stats_copy(half, k).start()

    blank = jnp.zeros((8, CH), jnp.float32)
    st_send[0] = conv_chunk(1, conv_chunk(0, blank))
    pair_copy(0).start()
    packed = conv_chunk(2, blank)
    send_chip_sums(0)
    st_send[1] = conv_chunk(3, packed)
    pair_copy(1).start()
    for k in range(1, RING):
        w1_send(0, k).wait_recv()
        w1_send(1, k).wait_recv()
    w_step(1)

    def block_of(c, off):
        return act.at[c, 2 * wrap(z + RING - off, RING) + core]

    def sib_block(c, off):
        return act.at[c, 2 * wrap(z + RING - off, RING) + 1 - core]

    HP = PX // 2

    def z_forward(c, off):
        ref = block_of(c, off)
        if off == 3:
            ref = ref.at[0:HP]
            return remote(ref, ref, zp_s.at[c, off], zr4.at[c, 0], up_z)
        return remote(ref, ref, zp_s.at[c, off], z_r.at[c, off], up_z)

    def z_backward(c, off):
        ref = block_of(c, RING - off if off else 0)
        if off == 3:
            ref = ref.at[HP:PX]
            return remote(ref, ref, zm_s.at[c, off], zr4.at[c, 1], down_z)
        return remote(ref, ref, zm_s.at[c, off], z_r.at[c, 3 + off], down_z)

    def sib_send(c, off):
        ref = block_of(c, off)
        return remote(ref, ref, sib_s.at[c, off], sib_r.at[c, off], sibling)

    gain = jnp.broadcast_to(vec_v[1:2, :], (8, CH))
    shift = jnp.broadcast_to(vec_v[2:3, :], (8, CH))

    for half in range(2):
        if half == 0:
            send_chip_sums(1)
        summed = st_chip[half]
        for k in range(1, RING):
            stats_copy(half, k).wait_recv()
            summed = summed + st_recv[half, k - 1]
        summed = summed / D
        mean = summed
        square = pltpu.roll(summed, 64, axis=1)
        rstd = lax.rsqrt(square - mean * mean + 1e-06)
        for c in (2 * half, 2 * half + 1):
            for q in range(PX // 16):
                parts = []
                for h in range(2):
                    lane = c * (PX // 8) + 2 * q + h
                    pick = lane % 64
                    m = jnp.broadcast_to(mean[:, pick : pick + 1], (8, CH))
                    r = jnp.broadcast_to(rstd[:, pick : pick + 1], (8, CH))
                    v = conv_v[lane * 8 : lane * 8 + 8, :]
                    parts.append((v - m) * r * gain + shift)
                act[c, col, 16 * q : 16 * q + 16, :] = jnp.concatenate(parts, axis=0).astype(
                    jnp.bfloat16
                )
            z_forward(c, 0).start()
            z_backward(c, 0).start()
            sib_send(c, 0).start()

    def relay(hop, c):
        if hop < 4:
            z_forward(c, hop - 1).wait_recv()
            z_forward(c, hop).start()
            sib_send(c, hop).start()
            z_backward(c, hop - 1).wait_recv()
            z_backward(c, hop).start()
            sib_send(c, RING - hop).start()
        else:
            z_forward(c, 3).wait_recv()
            z_backward(c, 3).wait_recv()
            sib_send(c, 4).start()

    def lhs(c, off):
        src = wrap(z + RING - off, RING)
        return [act[c, 2 * src], act[c, 2 * src + 1]]

    def rhs(ref, off):
        src = wrap(z + RING - off, RING)
        return ref[src].reshape(RING * SIDE, HALF)

    def multiply(c, offs, first):
        for off in offs:
            sib_send(c, off).wait_recv()
        left = []
        for off in offs:
            left += lhs(c, off)
        left = jnp.concatenate(left, axis=1)
        for which, ref in ((0, wa), (1, wb)):
            right = jnp.concatenate([rhs(ref, off) for off in offs], axis=0)
            prod = jnp.dot(left, right, preferred_element_type=jnp.float32)
            lanes = slice(which * HALF, (which + 1) * HALF)
            if first:
                acc[c, :, lanes] = prod
            else:
                acc[c, :, lanes] += prod

    hidden_bias = bin_v[0:1, :]
    ROWS = 64

    def finish(c):
        multiply(c, [4], False)

        def rows(i, _):
            at = pl.ds(pl.multiple_of(i * ROWS, ROWS), ROWS)
            v = acc[c, at, :] + hidden_bias
            obuf[c, at, :] = (0.5 * v * (1.0 + lax.erf(v * 0.7071067811865476))).astype(
                jnp.bfloat16
            )
            return 0

        lax.fori_loop(0, PX // ROWS, rows, 0)
        out_copy(c).start()

    def out_copy(c):
        return pltpu.make_async_copy(
            obuf.at[c], out_hbm.at[pl.ds(pl.multiple_of(c * PX, PX), PX)], out_s.at[c]
        )

    relay(1, 0)
    w_step(2)
    relay(1, 1)
    relay(1, 2)
    relay(1, 3)
    w_step(3)
    relay(2, 0)
    relay(2, 1)
    w_step(4)
    relay(2, 2)
    relay(2, 3)
    w_step(5)
    relay(3, 0)
    multiply(0, [0, 1, 7, 2, 6], True)

    def third(c, _):
        relay(3, c)
        multiply(c, [0, 1, 7, 2, 6], True)
        multiply(c - 1, [3, 5], False)
        return 0

    lax.fori_loop(1, NC, third, 0)
    relay(4, 0)
    multiply(NC - 1, [3, 5], False)

    def fourth(c, _):
        relay(4, c)
        finish(c - 1)
        return 0

    lax.fori_loop(1, NC, fourth, 0)
    finish(NC - 1)

    for c in halo:
        c.wait_send()
    for k in range(1, RING):
        w1_send(0, k).wait_send()
        w1_send(1, k).wait_send()
    for hop in range(1, 5):
        for which in range(2):
            for forward in (True, False):
                w_send(which, forward, hop).wait_send()
    for half in range(2):
        pair_copy(half).wait_send()
        for k in range(1, RING):
            stats_copy(half, k).wait_send()

    def drain(c, _):
        for off in range(4):
            z_forward(c, off).wait_send()
            z_backward(c, off).wait_send()
        for off in range(RING):
            sib_send(c, off).wait_send()
        out_copy(c).wait()
        return 0

    lax.fori_loop(0, NC, drain, 0)


def per_device(tokens, turns, dw_weight, dw_bias, ln_gain, ln_bias, w_in, b_in):
    pixels = SIDE * SIDE
    anywhere = pl.BlockSpec(memory_space=pl.ANY)
    hbm = pl.BlockSpec(memory_space=pltpu.HBM)
    dma = pltpu.SemaphoreType.DMA
    out = pl.pallas_call(
        body,
        name="block",
        out_shape=jax.ShapeDtypeStruct((pixels, HID), jnp.bfloat16),
        in_specs=[hbm] * 8,
        out_specs=anywhere,
        scratch_shapes=[
            pltpu.SMEM((4, 64), jnp.int32),
            pltpu.VMEM((pixels, CH), jnp.bfloat16),
            pltpu.VMEM((KERNEL * KERNEL, CH), jnp.float32),
            pltpu.VMEM((3, CH), jnp.float32),
            pltpu.VMEM((1, HID), jnp.float32),
            pltpu.VMEM((KERNEL * KERNEL, 8, CH), jnp.float32),
            pltpu.VMEM((38 * PITCH, CH), jnp.float32),
            pltpu.VMEM((4, 3 * SIDE, CH), jnp.bfloat16),
            pltpu.VMEM((4, 3 * SIDE, CH), jnp.bfloat16),
            pltpu.VMEM((pixels, CH), jnp.float32),
            pltpu.VMEM((2, 8, CH), jnp.float32),
            pltpu.VMEM((2, 8, CH), jnp.float32),
            pltpu.VMEM((2, 8, CH), jnp.float32),
            pltpu.VMEM((2, 7, 8, CH), jnp.float32),
            pltpu.VMEM((NC, 16, PX, CH), jnp.bfloat16),
            pltpu.VMEM((NC, PX, HID), jnp.float32),
            pltpu.VMEM((RING, RING, 32, HALF), jnp.bfloat16),
            pltpu.VMEM((RING, RING, 32, HALF), jnp.bfloat16),
            pltpu.VMEM((NC, PX, HID), jnp.bfloat16),
            dma((9,)),
            dma((4,)), dma((4,)),
            dma((2,)), dma((2,)),
            dma((2, 7)), dma((2, 7)),
            dma((2, 7)), dma((2, 7)),
            dma((2, 2, 4)), dma((2, 2, 4)),
            dma((NC, 4)), dma((NC, 4)), dma((NC, 6)), dma((NC, 2)),
            dma((NC, RING)), dma((NC, RING)),
            dma((NC,)),
        ],
        compiler_params=pltpu.CompilerParams(
            collective_id=0, has_side_effects=True, vmem_limit_bytes=40 * 1024 * 1024
        ),
    )(
        *[
            pltpu.with_memory_space_constraint(v, pltpu.HBM)
            for v in (
                turns.T,
                tokens.reshape(pixels, CH),
                dw_weight,
                dw_bias.reshape(1, CH),
                ln_gain.reshape(1, CH),
                ln_bias.reshape(1, CH),
                b_in.reshape(1, HID),
                w_in,
            )
        ]
    )
    return out.reshape(1, SIDE, SIDE, HID)


def solution(mesh):
    in_specs = (
        P("row", None, None, "col"),
        P(),
        P(None, "col"),
        P("col"),
        P("col"),
        P("col"),
        P("row", "col"),
        P("col"),
    )
    out_specs = P("row", None, None, "col")
    return jax.shard_map(
        per_device, mesh=mesh, in_specs=in_specs, out_specs=out_specs, check_vma=False
    )
```

```python
import functools

import jax
import jax.numpy as jnp
from jax import lax
from jax.experimental import pallas as pl
from jax.experimental.pallas import tpu as pltpu
from jax.sharding import PartitionSpec as P

D = 2048
KERNEL = 7
SIDE = 32
CH = 128
HID = 512
HALF = HID // 2
PITCH = 48
LEFT = 8
RING = 8
NC = 4
CROWS = SIDE // NC
PX = SIDE * SIDE // NC
MESH = pl.DeviceIdType.MESH


def body(
    turns_hbm, tok_hbm, dww_hbm, bias_hbm, gain_hbm, shift_hbm, bin_hbm, w_hbm, out_hbm,
    turns_ref, tok_v, dww_v, vec_v, bin_v, wexp, pad, sbuf, rbuf, conv_v,
    st_send, st_pair, st_chip, st_recv, act, acc, wa, wb, obuf,
    loc_sem, halo_s, halo_r, pair_s, pair_r, st_s, st_r, w1_s, w1_r, w2_s, w2_r,
    zp_s, zm_s, z_r, zr4, sib_s, sib_r, out_s,
):
    row = lax.axis_index("row")
    col = lax.axis_index("col")
    y, x = lax.div(row, RING), lax.rem(row, RING)
    z, core = lax.div(col, 2), lax.rem(col, 2)

    def wrap(v, n):
        return lax.rem(v, n)

    def remote(src, dst, ssem, rsem, dev):
        return pltpu.make_async_remote_copy(
            src_ref=src, dst_ref=dst, send_sem=ssem, recv_sem=rsem,
            device_id=dev, device_id_type=MESH,
        )

    x_peer = [(y * RING + wrap(x + k, RING), col) for k in range(RING)]
    y_peer = [(wrap(row + RING * k, 64), col) for k in range(RING)]
    z_line = [(row, wrap(col + k, 16)) for k in range(16)]
    up_z = (row, wrap(col + 2, 16))
    down_z = (row, wrap(col + 14, 16))
    sibling = (row, z * 2 + (1 - core))
    halo_dev = [
        (wrap(row + 8, 64), col),
        (wrap(row + 63, 64), col),
        (wrap(row + 56, 64), col),
        (wrap(row + 1, 64), col),
    ]
    peers = x_peer[1:] + y_peer[1:] + z_line[2::2] + [sibling, halo_dev[1], halo_dev[3]]

    barrier = pltpu.get_barrier_semaphore()
    for dev in peers:
        pl.semaphore_signal(barrier, inc=1, device_id=dev, device_id_type=MESH)

    loads = [
        pltpu.make_async_copy(tok_hbm, tok_v, loc_sem.at[0]),
        pltpu.make_async_copy(dww_hbm, dww_v, loc_sem.at[1]),
        pltpu.make_async_copy(bias_hbm, vec_v.at[0:1], loc_sem.at[2]),
        pltpu.make_async_copy(bin_hbm, bin_v, loc_sem.at[3]),
        pltpu.make_async_copy(w_hbm.at[:, 0:HALF], wa.at[y, x], loc_sem.at[4]),
        pltpu.make_async_copy(w_hbm.at[:, HALF:HID], wb.at[y, x], loc_sem.at[5]),
        pltpu.make_async_copy(gain_hbm, vec_v.at[1:2], loc_sem.at[6]),
        pltpu.make_async_copy(shift_hbm, vec_v.at[2:3], loc_sem.at[7]),
        pltpu.make_async_copy(turns_hbm, turns_ref, loc_sem.at[8]),
    ]
    for c in loads:
        c.start()

    zero_rows = jnp.zeros((3 * PITCH, CH), jnp.float32)
    pad[0 : 3 * PITCH, :] = zero_rows
    pad[35 * PITCH : 38 * PITCH, :] = zero_rows

    loads[0].wait()
    loads[8].wait()
    for i in range(SIDE):
        pad[(3 + i) * PITCH + LEFT : (3 + i) * PITCH + LEFT + SIDE, :] = tok_v[
            i * SIDE : (i + 1) * SIDE, :
        ].astype(jnp.float32)

    strips = [[], [], [], []]
    for d in range(3):
        strips[0].append(pad[pl.ds((3 + d) * PITCH + LEFT, SIDE), :])
        strips[1].append(pad[pl.ds(3 * PITCH + LEFT + 31 - d, SIDE, stride=PITCH), :])
        strips[2].append(pad[pl.ds((34 - d) * PITCH + LEFT, SIDE), :])
        strips[3].append(pad[pl.ds(3 * PITCH + LEFT + d, SIDE, stride=PITCH), :])
    chosen = []
    codes = []
    for s in range(4):
        code = turns_ref[s, halo_dev[s][0]]
        codes.append(code)
        k = lax.rem(s + 2 + code, 4)
        for d in range(3):
            chosen.append(
                jnp.where(
                    k == 0,
                    strips[0][d],
                    jnp.where(k == 1, strips[1][d], jnp.where(k == 2, strips[2][d], strips[3][d])),
                )
            )
    flip = (
        lax.broadcasted_iota(jnp.int32, (SIDE, SIDE), 0)
        + lax.broadcasted_iota(jnp.int32, (SIDE, SIDE), 1)
        == SIDE - 1
    )
    flip = jnp.where(flip, 1.0, 0.0).astype(jnp.bfloat16)
    side_by_side = jnp.concatenate(chosen, axis=1)
    flipped = jnp.dot(
        flip, side_by_side.astype(jnp.bfloat16), preferred_element_type=jnp.float32
    )
    for s in range(4):
        for d in range(3):
            q = 3 * s + d
            sbuf[s, d * SIDE : (d + 1) * SIDE, :] = jnp.where(
                codes[s] >= 4, flipped[:, q * CH : (q + 1) * CH], chosen[q]
            ).astype(jnp.bfloat16)

    pl.semaphore_wait(barrier, len(peers))

    halo = [
        remote(sbuf.at[s], rbuf.at[s], halo_s.at[s], halo_r.at[s], halo_dev[s])
        for s in range(4)
    ]
    for c in halo:
        c.start()
    here = (y, x)
    ahead = (y_peer[1], x_peer[1])
    behind = (y_peer[7], x_peer[7])

    def w1_send(which, k):
        ref = wa.at[y, x] if which == 0 else wb.at[y, x]
        dev = x_peer[k] if which == 0 else y_peer[k]
        return remote(ref, ref, w1_s.at[which, k - 1], w1_r.at[which, k - 1], dev)

    def w_group(which, g):
        return wa.at[g] if which == 0 else wb.at[:, g]

    def w_part(which, g, part):
        if which == 0:
            return wa.at[g, 4 * part : 4 * part + 4]
        return wb.at[4 * part : 4 * part + 4, g]

    def w_send(which, forward, hop):
        off = hop - 1
        if forward:
            g = wrap(here[which] + RING - off, RING)
            dev, lane = ahead[which], 0
        else:
            g = wrap(here[which] + off, RING)
            dev, lane = behind[which], 1
        ref = w_group(which, g) if hop < 4 else w_part(which, g, lane)
        return remote(
            ref, ref, w2_s.at[which, lane, hop - 1], w2_r.at[which, lane, hop - 1], dev
        )

    def w_step(hop):
        for which in range(2):
            for forward in (True, False):
                if hop > 1:
                    w_send(which, forward, hop - 1).wait_recv()
                if hop <= 4:
                    w_send(which, forward, hop).start()

    loads[4].wait()
    loads[5].wait()
    for k in range(1, RING):
        w1_send(0, k).start()
        w1_send(1, k).start()

    loads[1].wait()
    loads[2].wait()
    loads[3].wait()
    loads[6].wait()
    loads[7].wait()
    for k in range(KERNEL * KERNEL):
        wexp[k] = jnp.broadcast_to(dww_v[k : k + 1, :], (8, CH))

    for s in range(4):
        halo[s].wait_recv()
    for d in range(3):
        pad[pl.ds((2 - d) * PITCH + LEFT, SIDE), :] = rbuf[
            0, d * SIDE : (d + 1) * SIDE, :
        ].astype(jnp.float32)
        pad[pl.ds((35 + d) * PITCH + LEFT, SIDE), :] = rbuf[
            2, d * SIDE : (d + 1) * SIDE, :
        ].astype(jnp.float32)
        pad[pl.ds(3 * PITCH + LEFT + SIDE + d, SIDE, stride=PITCH), :] = rbuf[
            1, d * SIDE : (d + 1) * SIDE, :
        ].astype(jnp.float32)
        pad[pl.ds(3 * PITCH + LEFT - 1 - d, SIDE, stride=PITCH), :] = rbuf[
            3, d * SIDE : (d + 1) * SIDE, :
        ].astype(jnp.float32)

    bias = jnp.broadcast_to(vec_v[0:1, :], (8, CH))
    lane_id = lax.broadcasted_iota(jnp.int32, (8, CH), 1)

    def conv_chunk(c, packed):
        def block(jb, packed):
            total = [bias] * CROWS
            for b in range(KERNEL):
                taps = [wexp[a * KERNEL + b] for a in range(KERNEL)]
                for r in range(CROWS + KERNEL - 1):
                    start = (c * CROWS + r) * PITCH + LEFT - 3 + b + jb * 8
                    line = pad[pl.ds(start, 8), :]
                    for a in range(max(0, r - CROWS + 1), min(KERNEL - 1, r) + 1):
                        total[r - a] = total[r - a] + line * taps[a]
            for r in range(CROWS):
                i = c * CROWS + r
                at = pl.multiple_of(i * SIDE + jb * 8, 8)
                conv_v[pl.ds(at, 8), :] = total[r]
                lane = (4 * i) % 64 + jb
                s1 = jnp.sum(total[r], axis=1, keepdims=True)
                s2 = jnp.sum(total[r] * total[r], axis=1, keepdims=True)
                packed = jnp.where(lane_id == lane, s1, packed)
                packed = jnp.where(lane_id == lane + 64, s2, packed)
            return packed

        return lax.fori_loop(0, SIDE // 8, block, packed)

    def pair_copy(half):
        return remote(
            st_send.at[half], st_pair.at[half], pair_s.at[half], pair_r.at[half], sibling
        )

    def stats_copy(half, k):
        return remote(
            st_chip.at[half], st_recv.at[half, k - 1], st_s.at[half, k - 1],
            st_r.at[half, k - 1], z_line[2 * k],
        )

    def send_chip_sums(half):
        pair_copy(half).wait_recv()
        st_chip[half] = st_send[half] + st_pair[half]
        for k in range(1, RING):
            stats_copy(half, k).start()

    blank = jnp.zeros((8, CH), jnp.float32)
    st_send[0] = conv_chunk(1, conv_chunk(0, blank))
    pair_copy(0).start()
    packed = conv_chunk(2, blank)
    send_chip_sums(0)
    st_send[1] = conv_chunk(3, packed)
    pair_copy(1).start()
    for k in range(1, RING):
        w1_send(0, k).wait_recv()
        w1_send(1, k).wait_recv()
    w_step(1)

    def block_of(c, off):
        return act.at[c, 2 * wrap(z + RING - off, RING) + core]

    def sib_block(c, off):
        return act.at[c, 2 * wrap(z + RING - off, RING) + 1 - core]

    HP = PX // 2

    def z_forward(c, off):
        ref = block_of(c, off)
        if off == 3:
            ref = ref.at[0:HP]
            return remote(ref, ref, zp_s.at[c, off], zr4.at[c, 0], up_z)
        return remote(ref, ref, zp_s.at[c, off], z_r.at[c, off], up_z)

    def z_backward(c, off):
        ref = block_of(c, RING - off if off else 0)
        if off == 3:
            ref = ref.at[HP:PX]
            return remote(ref, ref, zm_s.at[c, off], zr4.at[c, 1], down_z)
        return remote(ref, ref, zm_s.at[c, off], z_r.at[c, 3 + off], down_z)

    def sib_send(c, off):
        ref = block_of(c, off)
        return remote(ref, ref, sib_s.at[c, off], sib_r.at[c, off], sibling)

    gain = jnp.broadcast_to(vec_v[1:2, :], (8, CH))
    shift = jnp.broadcast_to(vec_v[2:3, :], (8, CH))

    for half in range(2):
        if half == 0:
            send_chip_sums(1)
        summed = st_chip[half]
        for k in range(1, RING):
            stats_copy(half, k).wait_recv()
            summed = summed + st_recv[half, k - 1]
        summed = summed / D
        mean = summed
        square = pltpu.roll(summed, 64, axis=1)
        rstd = lax.rsqrt(square - mean * mean + 1e-06)
        for c in (2 * half, 2 * half + 1):
            for q in range(PX // 16):
                parts = []
                for h in range(2):
                    lane = c * (PX // 8) + 2 * q + h
                    pick = lane % 64
                    m = jnp.broadcast_to(mean[:, pick : pick + 1], (8, CH))
                    r = jnp.broadcast_to(rstd[:, pick : pick + 1], (8, CH))
                    v = conv_v[lane * 8 : lane * 8 + 8, :]
                    parts.append((v - m) * r * gain + shift)
                act[c, col, 16 * q : 16 * q + 16, :] = jnp.concatenate(parts, axis=0).astype(
                    jnp.bfloat16
                )
            z_forward(c, 0).start()
            z_backward(c, 0).start()
            sib_send(c, 0).start()

    def relay(hop, c):
        if hop < 4:
            z_forward(c, hop - 1).wait_recv()
            z_forward(c, hop).start()
            z_backward(c, hop - 1).wait_recv()
            z_backward(c, hop).start()
            sib_send(c, hop).start()
            sib_send(c, RING - hop).start()
        else:
            z_forward(c, 3).wait_recv()
            z_backward(c, 3).wait_recv()
            sib_send(c, 4).start()

    def lhs(c, off):
        src = wrap(z + RING - off, RING)
        return [act[c, 2 * src], act[c, 2 * src + 1]]

    def rhs(ref, off):
        src = wrap(z + RING - off, RING)
        return ref[src].reshape(RING * SIDE, HALF)

    def multiply(c, offs, first):
        for off in offs:
            sib_send(c, off).wait_recv()
        left = []
        for off in offs:
            left += lhs(c, off)
        left = jnp.concatenate(left, axis=1)
        for which, ref in ((0, wa), (1, wb)):
            right = jnp.concatenate([rhs(ref, off) for off in offs], axis=0)
            prod = jnp.dot(left, right, preferred_element_type=jnp.float32)
            lanes = slice(which * HALF, (which + 1) * HALF)
            if first:
                acc[c, :, lanes] = prod
            else:
                acc[c, :, lanes] += prod

    hidden_bias = bin_v[0:1, :]
    ROWS = 64

    def finish(c):
        multiply(c, [4], False)

        def rows(i, _):
            at = pl.ds(pl.multiple_of(i * ROWS, ROWS), ROWS)
            v = acc[c, at, :] + hidden_bias
            obuf[c, at, :] = (0.5 * v * (1.0 + lax.erf(v * 0.7071067811865476))).astype(
                jnp.bfloat16
            )
            return 0

        lax.fori_loop(0, PX // ROWS, rows, 0)
        out_copy(c).start()

    def out_copy(c):
        return pltpu.make_async_copy(
            obuf.at[c], out_hbm.at[pl.ds(pl.multiple_of(c * PX, PX), PX)], out_s.at[c]
        )

    relay(1, 0)
    w_step(2)
    relay(1, 1)
    relay(1, 2)
    relay(1, 3)
    w_step(3)
    relay(2, 0)
    relay(2, 1)
    w_step(4)
    for copy in halo:
        copy.wait_send()
    for k in range(1, RING):
        w1_send(0, k).wait_send()
        w1_send(1, k).wait_send()
    for half in range(2):
        pair_copy(half).wait_send()
        for k in range(1, RING):
            stats_copy(half, k).wait_send()
    relay(2, 2)
    relay(2, 3)
    w_step(5)
    relay(3, 0)
    for hop in range(1, 4):
        for which in range(2):
            w_send(which, True, hop).wait_send()
            w_send(which, False, hop).wait_send()
    multiply(0, [0, 1, 7, 2, 6], True)

    def third(c, _):
        for off in range(2):
            z_forward(c, off).wait_send()
            z_backward(c, off).wait_send()
        for off in (0, 1, 7):
            sib_send(c, off).wait_send()
        relay(3, c)
        multiply(c, [0, 1, 7, 2, 6], True)
        multiply(c - 1, [3, 5], False)
        return 0

    lax.fori_loop(1, NC, third, 0)
    relay(4, 0)
    for off in range(3):
        z_forward(0, off).wait_send()
        z_backward(0, off).wait_send()
    for off in (0, 1, 2, 6, 7):
        sib_send(0, off).wait_send()
    multiply(NC - 1, [3, 5], False)

    def fourth(c, _):
        z_forward(c, 2).wait_send()
        z_backward(c, 2).wait_send()
        for off in (2, 6):
            sib_send(c, off).wait_send()
        relay(4, c)
        finish(c - 1)
        return 0

    lax.fori_loop(1, NC, fourth, 0)
    finish(NC - 1)

    for which in range(2):
        w_send(which, True, 4).wait_send()
        w_send(which, False, 4).wait_send()

    def drain(c, _):
        z_forward(c, 3).wait_send()
        z_backward(c, 3).wait_send()
        for off in (3, 4, 5):
            sib_send(c, off).wait_send()
        out_copy(c).wait()
        return 0

    lax.fori_loop(0, NC, drain, 0)


def per_device(tokens, turns, dw_weight, dw_bias, ln_gain, ln_bias, w_in, b_in):
    pixels = SIDE * SIDE
    anywhere = pl.BlockSpec(memory_space=pl.ANY)
    hbm = pl.BlockSpec(memory_space=pltpu.HBM)
    dma = pltpu.SemaphoreType.DMA
    out = pl.pallas_call(
        body,
        name="block",
        out_shape=jax.ShapeDtypeStruct((pixels, HID), jnp.bfloat16),
        in_specs=[hbm] * 8,
        out_specs=anywhere,
        scratch_shapes=[
            pltpu.SMEM((4, 64), jnp.int32),
            pltpu.VMEM((pixels, CH), jnp.bfloat16),
            pltpu.VMEM((KERNEL * KERNEL, CH), jnp.float32),
            pltpu.VMEM((3, CH), jnp.float32),
            pltpu.VMEM((1, HID), jnp.float32),
            pltpu.VMEM((KERNEL * KERNEL, 8, CH), jnp.float32),
            pltpu.VMEM((38 * PITCH, CH), jnp.float32),
            pltpu.VMEM((4, 3 * SIDE, CH), jnp.bfloat16),
            pltpu.VMEM((4, 3 * SIDE, CH), jnp.bfloat16),
            pltpu.VMEM((pixels, CH), jnp.float32),
            pltpu.VMEM((2, 8, CH), jnp.float32),
            pltpu.VMEM((2, 8, CH), jnp.float32),
            pltpu.VMEM((2, 8, CH), jnp.float32),
            pltpu.VMEM((2, 7, 8, CH), jnp.float32),
            pltpu.VMEM((NC, 16, PX, CH), jnp.bfloat16),
            pltpu.VMEM((NC, PX, HID), jnp.float32),
            pltpu.VMEM((RING, RING, 32, HALF), jnp.bfloat16),
            pltpu.VMEM((RING, RING, 32, HALF), jnp.bfloat16),
            pltpu.VMEM((NC, PX, HID), jnp.bfloat16),
            dma((9,)),
            dma((4,)), dma((4,)),
            dma((2,)), dma((2,)),
            dma((2, 7)), dma((2, 7)),
            dma((2, 7)), dma((2, 7)),
            dma((2, 2, 4)), dma((2, 2, 4)),
            dma((NC, 4)), dma((NC, 4)), dma((NC, 6)), dma((NC, 2)),
            dma((NC, RING)), dma((NC, RING)),
            dma((NC,)),
        ],
        compiler_params=pltpu.CompilerParams(
            collective_id=0, has_side_effects=True, vmem_limit_bytes=40 * 1024 * 1024
        ),
    )(
        *[
            pltpu.with_memory_space_constraint(v, pltpu.HBM)
            for v in (
                turns.T,
                tokens.reshape(pixels, CH),
                dw_weight,
                dw_bias.reshape(1, CH),
                ln_gain.reshape(1, CH),
                ln_bias.reshape(1, CH),
                b_in.reshape(1, HID),
                w_in,
            )
        ]
    )
    return out.reshape(1, SIDE, SIDE, HID)


def solution(mesh):
    in_specs = (
        P("row", None, None, "col"),
        P(),
        P(None, "col"),
        P("col"),
        P("col"),
        P("col"),
        P("row", "col"),
        P("col"),
    )
    out_specs = P("row", None, None, "col")
    return jax.shard_map(
        per_device, mesh=mesh, in_specs=in_specs, out_specs=out_specs, check_vma=False
    )
```
